1024 devices in a mesh: ctx: 128 (over x_hi, z, core), tp: 8 (over x_lo, y).
Axes of the slice: x: 4 (x_hi: 2, x_lo: 2; x = x_hi * 2 + x_lo), y: 4, z: 32, core: 2. Of those that a mesh axis runs over, the one named last changes fastest.
Arguments:
- queries: bfloat16 [49152, 16, 128], P('ctx', 'tp'), may hold values from -6 to 6
- key_tensor: bfloat16 [49152, 2, 128], P('ctx'), may hold values from -6 to 6
- value_tensor: bfloat16 [49152, 2, 128], P('ctx'), may hold values from -6 to 6
- attn_output: bfloat16 [49152, 16, 128], P('ctx', 'tp'), may hold values from -4 to 4
- logsumexp_rows: float32 [16, 49152], P('tp', 'ctx'), may hold values from 4 to 7
- grad_output: bfloat16 [49152, 8192], P(('ctx', 'tp')), may hold values from -6 to 6
- out_proj: bfloat16 [2048, 8192], P('tp'), may hold values from -0.0625 to 0.0625
- block_doc: int32 [384], replicated, may hold values from 0 to 95, never falling along the last dimension, each value on 1 to 12 neighbouring positions
Outputs:
- grad_query: bfloat16 [49152, 16, 128], P('ctx', 'tp')
- grad_key: bfloat16 [49152, 2, 128], P(('ctx', 'tp'))
- grad_value: bfloat16 [49152, 2, 128], P(('ctx', 'tp'))
The draws below stay inside these ranges and needn't reach their ends.
Inputs may be any that keep to these rules, and one draw needn't show every extreme that they name: `block_doc`: document ids never fall along the sequence; one document spans 1 to 12 blocks, and some document spans exactly 12 in every draw.
All inputs are finite; a program needn't handle non-finite values.
Results may differ from the reference program's by a relative error of at most 0.012.
Values may be sent and summed in bfloat16 or wider, within the bound.
A program may use at most 32 MiB of HBM per device.

```python
import math
import jax
import jax.numpy as jnp
import numpy as np
from jax import lax

D = 8192
HEAD_SIZE = 128
QUERY_HEADS = 16
KEY_VALUE_HEADS = 2
TOKENS_PER_SHARD = 384
DOCBLK = 128
SPAN = 4
SEQUENCE_TOKENS = 49152
NBLK = 384
MOST_BLOCKS = 12


def block_scale(key, extent, shards, least, top_value):
    factor_of, own = 1.0, jax.random.fold_in(key, 6)
    for dim, blocks in shards:
        steps = jnp.exp(jax.random.uniform(jax.random.fold_in(own, dim), (blocks,), jnp.float32, least / len(shards), top_value / len(shards)))
        factor_of = factor_of * jnp.repeat(steps, extent[dim] // blocks).reshape([-1 if axis == dim else 1 for axis in range(len(extent))])
    return factor_of


def profile(number_of, total, bound, lean):
    loads = [(1 << 20) // math.isqrt(rank ** lean) + 1 for rank in range(2, number_of + 1)]
    surplus, holding = total - bound - (number_of - 1), [1] * (number_of - 1)
    while surplus > 0:
        free = [i for i in range(number_of - 1) if holding[i] < bound]
        whole, left = sum([loads[i] for i in free]), surplus
        for i in free:
            extra = min(bound - holding[i], max(1, left * loads[i] // whole), surplus)
            holding[i] = holding[i] + extra
            surplus = surplus - extra
    return np.array([bound] + holding)


def uneven_parts(stream_key, count, total, most, slope):
    if count == 2:
        one = jax.random.randint(stream_key, (), max(1, total - most), min(most, total - 1) + 1)
        return jnp.stack([one, total - one])
    tallies = jnp.asarray(profile(count, total, most, slope), jnp.int32)
    couples = (count - 1) // 2
    giver, receiver = tallies[1:1 + 2 * couples:2], tallies[2:2 + 2 * couples:2]
    room = jnp.minimum(giver - 1, most - receiver)
    shifted = jax.random.randint(jax.random.fold_in(stream_key, 1), (couples,), 0, 1 << 20) % (room + 1)
    tallies = tallies.at[1:1 + 2 * couples:2].set(giver - shifted).at[2:2 + 2 * couples:2].set(receiver + shifted)
    return tallies[jax.random.permutation(jax.random.fold_in(stream_key, 2), count)]


def normal_values(key, extent, spread, limit, shards=(), kind=jnp.bfloat16):
    result = jax.random.normal(key, extent, jnp.float32) * spread
    if len(shards) > 0:
        result = block_scale(key, extent, shards, -0.22, 0.18) * result
    return jnp.clip(result, min=-limit, max=limit).astype(kind)


def setup_inputs(seed: int = 0) -> dict:
    seeds = jax.random.split(jax.random.key(seed), 9)
    return {
        "queries": normal_values(seeds[0], (SEQUENCE_TOKENS, QUERY_HEADS, HEAD_SIZE), 1.0, 6.0, ((0, 128), (1, 8))),
        "key_tensor": normal_values(seeds[1], (SEQUENCE_TOKENS, KEY_VALUE_HEADS, HEAD_SIZE), 1.0, 6.0, ((0, 128),)),
        "value_tensor": normal_values(seeds[2], (SEQUENCE_TOKENS, KEY_VALUE_HEADS, HEAD_SIZE), 1.0, 6.0, ((0, 128),)),
        "attn_output": normal_values(seeds[3], (SEQUENCE_TOKENS, QUERY_HEADS, HEAD_SIZE), 0.3, 4.0, ((0, 128), (1, 8))),
        "logsumexp_rows": jnp.clip(4.0 + 3.0 * jax.random.uniform(seeds[4], (QUERY_HEADS, SEQUENCE_TOKENS), jnp.float32) ** block_scale(seeds[4], (QUERY_HEADS, SEQUENCE_TOKENS), ((0, 8), (1, 128)), -0.2, 0.2), 4.0, 7.0),
        "grad_output": normal_values(seeds[5], (SEQUENCE_TOKENS, D), 1.0, 6.0, ((0, 1024),)),
        "out_proj": normal_values(seeds[6], (QUERY_HEADS * HEAD_SIZE, D), D ** -0.5, 0.0625, ((0, 8),)),
        "block_doc": jnp.searchsorted(jnp.cumsum(uneven_parts(seeds[7], NBLK // 4, NBLK, MOST_BLOCKS, 2)), jnp.arange(NBLK), side="right").astype(jnp.int32),
    }


def reference(queries, key_tensor, value_tensor, attn_output, logsumexp_rows, grad_output, out_proj, block_doc):
    single_float = jnp.float32
    query_group = QUERY_HEADS // KEY_VALUE_HEADS
    head_window = SPAN * TOKENS_PER_SHARD
    score_scale = HEAD_SIZE ** -0.5
    head_gradients = jnp.dot(grad_output, out_proj.T, preferred_element_type=single_float).astype(jnp.bfloat16)
    head_gradients = head_gradients.reshape(SEQUENCE_TOKENS, QUERY_HEADS, HEAD_SIZE)
    delta_terms = jnp.sum(head_gradients.astype(single_float) * attn_output.astype(single_float), axis=2)
    positions = jnp.arange(SEQUENCE_TOKENS, dtype=jnp.int32)
    token_doc = block_doc[positions // DOCBLK]
    doc_pad = jnp.concatenate([jnp.full((head_window,), -1, jnp.int32), token_doc])
    pos_pad = jnp.arange(SEQUENCE_TOKENS + head_window, dtype=jnp.int32) - head_window
    key_pad = jnp.pad(key_tensor.astype(single_float), ((head_window, 0), (0, 0), (0, 0)))
    value_pad = jnp.pad(value_tensor.astype(single_float), ((head_window, 0), (0, 0), (0, 0)))
    span_rows = head_window + TOKENS_PER_SHARD

    def one_block(carry, block_index):
        key_acc, value_acc = carry
        first_row_index = (block_index * TOKENS_PER_SHARD).astype(jnp.int32)
        query_block = lax.dynamic_slice_in_dim(queries, first_row_index, TOKENS_PER_SHARD, 0).astype(single_float).reshape(TOKENS_PER_SHARD, KEY_VALUE_HEADS, query_group, HEAD_SIZE)
        gradient_block = lax.dynamic_slice_in_dim(head_gradients, first_row_index, TOKENS_PER_SHARD, 0).astype(single_float).reshape(TOKENS_PER_SHARD, KEY_VALUE_HEADS, query_group, HEAD_SIZE)
        logsumexp_block = lax.dynamic_slice_in_dim(logsumexp_rows, first_row_index, TOKENS_PER_SHARD, 1).reshape(KEY_VALUE_HEADS, query_group, TOKENS_PER_SHARD)
        delta_block = lax.dynamic_slice_in_dim(delta_terms, first_row_index, TOKENS_PER_SHARD, 0).T.reshape(KEY_VALUE_HEADS, query_group, TOKENS_PER_SHARD)
        key_win = lax.dynamic_slice_in_dim(key_pad, first_row_index, span_rows, 0)
        value_win = lax.dynamic_slice_in_dim(value_pad, first_row_index, span_rows, 0)
        key_pos = lax.dynamic_slice_in_dim(pos_pad, first_row_index, span_rows, 0)
        key_doc = lax.dynamic_slice_in_dim(doc_pad, first_row_index, span_rows, 0)
        query_pos = first_row_index + jnp.arange(TOKENS_PER_SHARD, dtype=jnp.int32)
        query_doc = lax.dynamic_slice_in_dim(token_doc, first_row_index, TOKENS_PER_SHARD, 0)
        allowed = (query_doc[:, None] == key_doc[None, :]) & (key_pos[None, :] <= query_pos[:, None])
        scores = jnp.einsum("igzd,jgd->gzij", query_block, key_win) * score_scale
        prob_full = jnp.exp(jnp.where(allowed[None, None], scores - logsumexp_block[..., None], -1e30))
        dprobs = jnp.einsum("igzd,jgd->gzij", gradient_block, value_win)
        dscores = (prob_full * (dprobs - delta_block[..., None]) * score_scale).astype(jnp.bfloat16)
        dscores = lax.optimization_barrier(dscores).astype(single_float)
        prob_low = lax.optimization_barrier(prob_full.astype(jnp.bfloat16)).astype(single_float)
        grad_q_blk = jnp.einsum("gzij,jgd->igzd", dscores, key_win).reshape(TOKENS_PER_SHARD, QUERY_HEADS, HEAD_SIZE)
        grad_k_win = jnp.einsum("gzij,igzd->jgd", dscores, query_block)
        grad_v_win = jnp.einsum("gzij,igzd->jgd", prob_low, gradient_block)
        old_key = lax.dynamic_slice_in_dim(key_acc, first_row_index, span_rows, 0)
        old_value = lax.dynamic_slice_in_dim(value_acc, first_row_index, span_rows, 0)
        key_acc = lax.dynamic_update_slice_in_dim(key_acc, old_key + grad_k_win, first_row_index, 0)
        value_acc = lax.dynamic_update_slice_in_dim(value_acc, old_value + grad_v_win, first_row_index, 0)
        return (key_acc, value_acc), grad_q_blk.astype(jnp.bfloat16)

    empty_accumulator = jnp.zeros((SEQUENCE_TOKENS + head_window, KEY_VALUE_HEADS, HEAD_SIZE), single_float)
    block_ids = jnp.arange(SEQUENCE_TOKENS // TOKENS_PER_SHARD, dtype=jnp.int32)
    (key_acc, value_acc), grad_q_all = lax.scan(one_block, (empty_accumulator, empty_accumulator), block_ids)
    grad_query = grad_q_all.reshape(SEQUENCE_TOKENS, QUERY_HEADS, HEAD_SIZE)
    grad_key = key_acc[head_window:].astype(jnp.bfloat16)
    grad_value = value_acc[head_window:].astype(jnp.bfloat16)
    return (grad_query, grad_key, grad_value)
```

```python
import functools

import jax
import jax.numpy as jnp
from jax import lax
from jax.experimental import pallas as pl
from jax.experimental.pallas import tpu as pltpu
from jax.sharding import PartitionSpec as P

F32 = jnp.float32
BF16 = jnp.bfloat16
MESH = pl.DeviceIdType.MESH
RANKS = 128
REACH = 4
ROWS = 384
PART = 48
HEAD = 128
WIDE = 256
D = 8192
HALF = D // 2
SUB = D // 8
NEG = -1e30
SCALE = HEAD ** -0.5
NT = (((1,), (1,)), ((), ()))


def ring_places():
    c = lax.axis_index("ctx")
    t = lax.axis_index("tp")
    return c, t


def gather_kernel(
    q_in, kv_in, lse_in, o_in, g_hbm, w_hbm,
    qw, kvw, lsew, dow, delw,
    wmine, woth, gbuf, xsend,
    loc_sem, g_ss, g_rs, w_ss, w_rs, s_ss, s_rs,
    q_ss, q_rs, l_ss, l_rs, kv_ss, kv_rs, x_ss, x_rs, do_ss, do_rs, de_ss, de_rs,
):
    c, t = ring_places()
    xlo = t // 4
    y = t % 4
    core = c % 2
    up = (c, xlo * 4 + (y + 1) % 4)
    down = (c, xlo * 4 + (y + 3) % 4)
    other = (t + 4) % 8
    lo = (c, other)
    hi = ((c + RANKS // 2) % RANKS, other)
    sib = (c + 1 - 2 * core, t)
    prev = ((c + RANKS - 1) % RANKS, t)
    nxt = ((c + 1) % RANKS, t)
    far = ((c + RANKS - 1 + 2 * core) % RANKS, t)

    barrier = pltpu.get_barrier_semaphore()
    for peer in (up, down, lo, hi, sib, far):
        pl.semaphore_signal(barrier, inc=1, device_id=peer, device_id_type=MESH)
    pl.semaphore_wait(barrier, 6)

    def remote(src, dst, ss, rs, peer):
        return pltpu.make_async_remote_copy(
            src_ref=src, dst_ref=dst, send_sem=ss, recv_sem=rs,
            device_id=peer, device_id_type=MESH,
        )

    A = pl.ds(0, HALF)
    B = pl.ds(HALF, HALF)

    def slot(s, cols):
        return gbuf.at[pl.ds(s * PART, PART), cols]

    g_up_a = remote(g_hbm.at[:, A], slot(1, A), g_ss.at[0], g_rs.at[0], up)
    g_up_b = remote(g_hbm.at[:, B], slot(1, B), g_ss.at[1], g_rs.at[1], up)
    g_up_f = remote(slot(1, A), slot(3, A), g_ss.at[2], g_rs.at[2], up)
    g_dn_b = remote(g_hbm.at[:, B], slot(2, B), g_ss.at[3], g_rs.at[3], down)
    g_dn_a = remote(g_hbm.at[:, A], slot(2, A), g_ss.at[4], g_rs.at[4], down)
    g_dn_f = remote(slot(2, B), slot(3, B), g_ss.at[5], g_rs.at[5], down)

    def wcols(link, k):
        return pl.ds(pl.multiple_of(core * 4096 + link * 2048 + k * SUB, SUB), SUB)

    w_sends, s_sends = [], []
    for k in range(2):
        for link, peer in ((0, lo), (1, hi)):
            i = 2 * k + link
            cols = wcols(link, k)
            w_sends.append(remote(w_hbm.at[:, cols], woth.at[:, cols], w_ss.at[i], w_rs.at[i], peer))
            s_sends.append(remote(woth.at[:, cols], woth.at[:, cols], s_ss.at[i], s_rs.at[i], sib))

    g_up_a.start()
    g_dn_b.start()
    w_sends[0].start()
    w_sends[1].start()
    g_up_b.start()
    g_dn_a.start()
    w_sends[2].start()
    w_sends[3].start()

    def back_ok(d):
        return jnp.logical_and(c >= 1, c + d <= RANKS - 1)

    def fwd_ok(d):
        return jnp.logical_and(c <= RANKS - 2, c - d >= 0)

    def q_copy(d):
        src = q_in if d == 0 else qw.at[d]
        return remote(src, qw.at[d + 1], q_ss.at[d], q_rs.at[d], prev)

    def l_copy(d):
        src = lse_in if d == 0 else lsew.at[d]
        return remote(src, lsew.at[d + 1], l_ss.at[d], l_rs.at[d], prev)

    def kv_copy(d):
        src = kv_in if d == 0 else kvw.at[d]
        return remote(src, kvw.at[d + 1], kv_ss.at[d], kv_rs.at[d], nxt)

    def do_copy(d, u):
        return remote(dow.at[d, u], dow.at[d + 1, u], do_ss.at[d, u], do_rs.at[d, u], prev)

    def de_copy(d):
        return remote(delw.at[d], delw.at[d + 1], de_ss.at[d], de_rs.at[d], prev)

    @pl.when(back_ok(0))
    def _():
        q_copy(0).start()
        l_copy(0).start()

    @pl.when(fwd_ok(0))
    def _():
        kv_copy(0).start()

    w_loc = pltpu.make_async_copy(w_hbm, wmine, loc_sem.at[0])
    g_loc = pltpu.make_async_copy(g_hbm, gbuf.at[pl.ds(0, PART), :], loc_sem.at[1])
    w_loc.start()
    g_loc.start()

    qw[0] = q_in[...]
    kvw[0] = kv_in[...]
    lsew[0] = lse_in[...]
    for d in range(1, REACH + 1):
        @pl.when(c + d > RANKS - 1)
        def _():
            qw[d] = jnp.zeros((ROWS, WIDE), BF16)
            lsew[d] = jnp.zeros((2, ROWS), F32)
            delw[d] = jnp.zeros((2, ROWS), F32)
            dow[d] = jnp.zeros((8, PART, WIDE), BF16)

        @pl.when(c - d < 0)
        def _():
            kvw[d] = jnp.zeros((ROWS, WIDE), BF16)

    def project(first, count, w):
        def body(k, acc):
            cols = pl.ds(pl.multiple_of(k * 1024, 1024), 1024)
            return acc + lax.dot_general(
                gbuf[first * PART:(first + count) * PART, cols], w[:, cols], NT,
                preferred_element_type=F32,
            )
        return lax.fori_loop(0, 8, body, jnp.zeros((count * PART, WIDE), F32)).astype(BF16)

    slot_y = (y, (y + 3) % 4, (y + 1) % 4, (y + 2) % 4)

    def mine(first, count):
        out = project(first, count, wmine)
        for s in range(first, first + count):
            dow[0, xlo * 4 + slot_y[s]] = out[(s - first) * PART:(s - first + 1) * PART]

    def x_copy(s):
        return remote(
            xsend.at[s], dow.at[0, xlo * 4 + slot_y[s]], x_ss.at[s], x_rs.at[s], lo)

    def theirs(first, count):
        out = project(first, count, woth)
        for s in range(first, first + count):
            xsend[s] = out[(s - first) * PART:(s - first + 1) * PART]
            x_copy(s).start()

    def chain_start(u):
        @pl.when(back_ok(0))
        def _():
            do_copy(0, u).start()

    def chain_forward(u):
        for d in range(1, REACH):
            @pl.when(c + d <= RANKS - 1)
            def _():
                do_copy(d - 1, u).wait_recv()

            @pl.when(back_ok(d))
            def _():
                do_copy(d, u).start()

    w_loc.wait()
    g_loc.wait()
    mine(0, 1)
    chain_start(xlo * 4 + slot_y[0])

    for d in range(1, REACH):
        @pl.when(c - d >= 0)
        def _():
            kv_copy(d - 1).wait_recv()

        @pl.when(fwd_ok(d))
        def _():
            kv_copy(d).start()

        @pl.when(c + d <= RANKS - 1)
        def _():
            q_copy(d - 1).wait_recv()
            l_copy(d - 1).wait_recv()

        @pl.when(back_ok(d))
        def _():
            q_copy(d).start()
            l_copy(d).start()

    g_up_a.wait_recv()
    g_up_f.start()
    g_dn_b.wait_recv()
    g_dn_f.start()
    for i in range(2):
        w_sends[i].wait_recv()
        s_sends[i].start()
    chain_forward(xlo * 4 + slot_y[0])
    g_up_b.wait_recv()
    g_dn_a.wait_recv()
    mine(1, 2)
    chain_start(xlo * 4 + slot_y[1])
    chain_start(xlo * 4 + slot_y[2])
    chain_forward(xlo * 4 + slot_y[1])
    chain_forward(xlo * 4 + slot_y[2])
    for i in range(2, 4):
        w_sends[i].wait_recv()
        s_sends[i].start()
    for i in range(4):
        s_sends[i].wait_recv()
    theirs(0, 3)
    g_up_f.wait_recv()
    g_dn_f.wait_recv()
    theirs(3, 1)
    mine(3, 1)
    chain_start(xlo * 4 + slot_y[3])
    for s in range(4):
        x_copy(s).wait_recv()
        chain_start((1 - xlo) * 4 + slot_y[s])

    ones = jnp.ones((8, HEAD), F32)
    for h in range(2):
        lanes = slice(h * HEAD, (h + 1) * HEAD)
        own = dow[0].reshape(ROWS, WIDE)[:, lanes].astype(F32)
        prod = own * o_in[:, lanes].astype(F32)
        row = lax.dot_general(ones, prod, NT, precision=lax.Precision.HIGHEST,
                              preferred_element_type=F32)
        delw[0, h:h + 1, :] = row[0:1]

    @pl.when(back_ok(0))
    def _():
        de_copy(0).start()

    chain_forward(xlo * 4 + slot_y[3])
    for s in range(4):
        chain_forward((1 - xlo) * 4 + slot_y[s])
    for d in range(1, REACH):
        @pl.when(c + d <= RANKS - 1)
        def _():
            de_copy(d - 1).wait_recv()

        @pl.when(back_ok(d))
        def _():
            de_copy(d).start()

    last = REACH - 1

    @pl.when(c + REACH <= RANKS - 1)
    def _():
        q_copy(last).wait_recv()
        l_copy(last).wait_recv()
        de_copy(last).wait_recv()
        for u in range(8):
            do_copy(last, u).wait_recv()

    @pl.when(c - REACH >= 0)
    def _():
        kv_copy(last).wait_recv()

    for cp in (g_up_a, g_up_b, g_up_f, g_dn_a, g_dn_b, g_dn_f, *w_sends, *s_sends):
        cp.wait_send()
    for s in range(4):
        x_copy(s).wait_send()
    for d in range(REACH):
        @pl.when(back_ok(d))
        def _():
            q_copy(d).wait_send()
            l_copy(d).wait_send()
            de_copy(d).wait_send()
            for u in range(8):
                do_copy(d, u).wait_send()

        @pl.when(fwd_ok(d))
        def _():
            kv_copy(d).wait_send()


def attend_kernel(
    qw, kvw, lsew, dow, delw, docs,
    dq_out, dkv_out,
    part, land, ss, rs,
):
    c, t = ring_places()
    xlo = t // 4
    barrier = pltpu.get_barrier_semaphore()
    for step in range(1, 8):
        pl.semaphore_signal(barrier, inc=1, device_id=(c, (t + step) % 8), device_id_type=MESH)
    pl.semaphore_wait(barrier, 7)

    lane_blk = lax.broadcasted_iota(jnp.int32, (1, ROWS), 1) // HEAD

    def doc_at(block):
        return docs[jnp.clip(block, 0, 3 * RANKS - 1)]

    def bias_row(mine, far_rank, first):
        vals = []
        for b in range(3):
            same = doc_at(far_rank * 3 + b) == mine
            ok = jnp.logical_and(same, jnp.logical_and(far_rank >= 0, far_rank < RANKS))
            vals.append(jnp.where(ok, 0.0, NEG).astype(F32))
        return jnp.where(lane_blk == 0, vals[0], jnp.where(lane_blk == 1, vals[1], vals[2]))

    for kb in range(3):
        k_doc = docs[c * 3 + kb]
        k = kvw[0, kb * HEAD:(kb + 1) * HEAD, 0:HEAD]
        v = kvw[0, kb * HEAD:(kb + 1) * HEAD, HEAD:WIDE]
        k_pos = lax.broadcasted_iota(jnp.int32, (HEAD, ROWS), 0) + kb * HEAD
        q_pos = lax.broadcasted_iota(jnp.int32, (HEAD, ROWS), 1)

        def step(d, carry, k=k, v=v, k_doc=k_doc, k_pos=k_pos, q_pos=q_pos):
            dk, dv = carry
            row = bias_row(k_doc, c + d, 0)
            causal = (k_pos <= q_pos + d * ROWS)
            for h in range(2):
                lanes = slice(h * HEAD, (h + 1) * HEAD)
                q = qw[d, :, lanes]
                do = dow[d, :, lanes]
                s = lax.dot_general(k, q, NT, preferred_element_type=F32)
                x = s * SCALE + (row - lsew[d, h:h + 1, :])
                p = jnp.exp(jnp.where(causal, x, NEG))
                dp = lax.dot_general(v, do, NT, preferred_element_type=F32)
                ds = (p * (dp - delw[d, h:h + 1, :]) * SCALE).astype(BF16)
                dk = dk + jnp.dot(ds, q, preferred_element_type=F32)
                dv = dv + jnp.dot(p.astype(BF16), do, preferred_element_type=F32)
            return dk, dv

        zero = jnp.zeros((HEAD, HEAD), F32)
        dk, dv = lax.fori_loop(0, REACH + 1, step, (zero, zero))
        part[kb * HEAD:(kb + 1) * HEAD, 0:HEAD] = dk.astype(BF16)
        part[kb * HEAD:(kb + 1) * HEAD, HEAD:WIDE] = dv.astype(BF16)

    def send(step):
        to = (t + step) % 8
        return pltpu.make_async_remote_copy(
            src_ref=part.at[pl.ds(pl.multiple_of(to * PART, PART), PART)],
            dst_ref=land.at[step],
            send_sem=ss.at[step], recv_sem=rs.at[step],
            device_id=(c, to), device_id_type=MESH)

    for step in range(1, 8):
        send(step).start()

    for h in range(2):
        lse_col = jnp.broadcast_to(lsew[0, h:h + 1, :], (HEAD, ROWS)).T
        del_col = jnp.broadcast_to(delw[0, h:h + 1, :], (HEAD, ROWS)).T
        lanes = slice(h * HEAD, (h + 1) * HEAD)
        for qb in range(3):
            q_doc = docs[c * 3 + qb]
            rows = slice(qb * HEAD, (qb + 1) * HEAD)
            q = qw[0, rows, lanes]
            do = dow[0, rows, lanes]
            lse = jnp.concatenate([lse_col[rows]] * 3, axis=1)
            dl = jnp.concatenate([del_col[rows]] * 3, axis=1)
            q_pos = lax.broadcasted_iota(jnp.int32, (HEAD, ROWS), 0) + qb * HEAD
            k_pos = lax.broadcasted_iota(jnp.int32, (HEAD, ROWS), 1)

            def step(d, dq, q=q, do=do, lse=lse, dl=dl, q_doc=q_doc, q_pos=q_pos, k_pos=k_pos):
                row = bias_row(q_doc, c - d, 0)
                k = kvw[d, :, 0:HEAD]
                v = kvw[d, :, HEAD:WIDE]
                s = lax.dot_general(q, k, NT, preferred_element_type=F32)
                x = s * SCALE + (row - lse)
                p = jnp.exp(jnp.where(k_pos <= q_pos + d * ROWS, x, NEG))
                dp = lax.dot_general(do, v, NT, preferred_element_type=F32)
                ds = (p * (dp - dl) * SCALE).astype(BF16)
                return dq + jnp.dot(ds, k, preferred_element_type=F32)

            dq = lax.fori_loop(0, REACH + 1, step, jnp.zeros((HEAD, HEAD), F32))
            dq_out[h, rows, :] = dq.astype(BF16)

    totals = [jnp.zeros((PART, WIDE), F32), jnp.zeros((PART, WIDE), F32)]
    own = part[pl.ds(pl.multiple_of(t * PART, PART), PART), :].astype(F32)
    for step in range(8):
        if step == 0:
            got = own
        else:
            send(step).wait_recv()
            got = land[step].astype(F32)
        src_lo = ((t + 8 - step) % 8) // 4
        w1 = src_lo.astype(F32)
        totals[0] = totals[0] + got * (1.0 - w1)
        totals[1] = totals[1] + got * w1
    for g in range(2):
        dkv_out[g] = totals[g].astype(BF16)
    for step in range(1, 8):
        send(step).wait_send()


def per_device(queries, key_tensor, value_tensor, attn_output, lse, grad_output, out_proj, block_doc):
    group = lax.axis_index("tp") // 4
    q2 = queries.reshape(ROWS, WIDE)
    o2 = attn_output.reshape(ROWS, WIDE)
    kv = jnp.concatenate(
        [
            lax.dynamic_index_in_dim(key_tensor, group, 1, keepdims=False),
            lax.dynamic_index_in_dim(value_tensor, group, 1, keepdims=False),
        ],
        axis=1,
    )
    vmem = pl.BlockSpec(memory_space=pltpu.VMEM)
    hbm = pl.BlockSpec(memory_space=pl.ANY)
    dma = pltpu.SemaphoreType.DMA
    span = REACH + 1
    qw, kvw, lsew, dow, delw = pl.pallas_call(
        gather_kernel,
        out_shape=(
            jax.ShapeDtypeStruct((span, ROWS, WIDE), BF16),
            jax.ShapeDtypeStruct((span, ROWS, WIDE), BF16),
            jax.ShapeDtypeStruct((span, 2, ROWS), F32),
            jax.ShapeDtypeStruct((span, 8, PART, WIDE), BF16),
            jax.ShapeDtypeStruct((span, 2, ROWS), F32),
        ),
        in_specs=[vmem, vmem, vmem, vmem, hbm, hbm],
        out_specs=(vmem,) * 5,
        scratch_shapes=[
            pltpu.VMEM((WIDE, D), BF16),
            pltpu.VMEM((WIDE, D), BF16),
            pltpu.VMEM((4 * PART, D), BF16),
            pltpu.VMEM((4, PART, WIDE), BF16),
            dma((2,)), dma((6,)), dma((6,)), dma((4,)), dma((4,)), dma((4,)), dma((4,)),
            dma((4,)), dma((4,)), dma((4,)), dma((4,)), dma((4,)), dma((4,)),
            dma((4,)), dma((4,)), dma((4, 8)), dma((4, 8)), dma((4,)), dma((4,)),
        ],
        compiler_params=pltpu.CompilerParams(
            collective_id=0, has_side_effects=True, vmem_limit_bytes=40 << 20),
        name="gather_project",
    )(q2, kv, lse, o2, grad_output, out_proj)
    dq, dkv = pl.pallas_call(
        attend_kernel,
        out_shape=(
            jax.ShapeDtypeStruct((2, ROWS, HEAD), BF16),
            jax.ShapeDtypeStruct((2, PART, WIDE), BF16),
        ),
        in_specs=[vmem] * 5 + [pl.BlockSpec(memory_space=pltpu.SMEM)],
        out_specs=(vmem, vmem),
        scratch_shapes=[
            pltpu.VMEM((ROWS, WIDE), BF16),
            pltpu.VMEM((8, PART, WIDE), BF16),
            dma((8,)), dma((8,)),
        ],
        compiler_params=pltpu.CompilerParams(
            collective_id=1, has_side_effects=True, vmem_limit_bytes=40 << 20),
        name="attend_reduce",
    )(qw, kvw, lsew, dow.reshape(span, ROWS, WIDE), delw, block_doc)
    grad_query = jnp.transpose(dq, (1, 0, 2))
    grad_key = jnp.transpose(dkv[:, :, :HEAD], (1, 0, 2))
    grad_value = jnp.transpose(dkv[:, :, HEAD:], (1, 0, 2))
    return grad_query, grad_key, grad_value


def solution(mesh):
    placed = (
        P("ctx", "tp", None),
        P("ctx", None, None),
        P("ctx", None, None),
        P("ctx", "tp", None),
        P("tp", "ctx"),
        P(("ctx", "tp"), None),
        P("tp", None),
        P(),
    )
    return jax.shard_map(
        per_device,
        mesh=mesh,
        in_specs=placed,
        out_specs=(
            P("ctx", "tp", None),
            P(("ctx", "tp"), None, None),
            P(("ctx", "tp"), None, None),
        ),
        check_vma=False,
    )
```

```python
import jax
import jax.numpy as jnp
from jax import lax
from jax.experimental import pallas as pl
from jax.experimental.pallas import tpu as pltpu
from jax.sharding import PartitionSpec as P

F32 = jnp.float32
BF16 = jnp.bfloat16
MESH = pl.DeviceIdType.MESH
RANKS = 128
REACH = 4
ROWS = 384
PART = 48
HEAD = 128
WIDE = 256
D = 8192
HALF = D // 2
QUARTER = D // 4
SUB = D // 8
NEG = -1e30
SCALE = HEAD ** -0.5
NT = (((1,), (1,)), ((), ()))


def ring_places():
    c = lax.axis_index("ctx")
    t = lax.axis_index("tp")
    return c, t


def fused_kernel(
    docs, q_in, kv_in, lse_in, o_hbm, g_hbm, w_hbm,
    dq_out, dkv_out,
    qw, kvw, lsew, dow, delw, o_in, lsec, delc,
    wmine, woth, gbuf, xsend, acc_t, acc_m, dk_acc, dv_acc, dq_acc, part, land,
    loc_sem, g_ss, g_rs, w_ss, w_rs, s_ss, s_rs,
    q_ss, q_rs, l_ss, l_rs, kv_ss, kv_rs, x_ss, x_rs, do_ss, do_rs, de_ss, de_rs,
    r_ss, r_rs, ready,
    rq, rl, rkv, rdo, rde, rq_rs, rl_rs, rkv_rs, rdo_rs, rde_rs,
):
    c, t = ring_places()
    xlo = t // 4
    y = t % 4
    core = c % 2
    up = (c, xlo * 4 + (y + 1) % 4)
    down = (c, xlo * 4 + (y + 3) % 4)
    other = (t + 4) % 8
    lo = (c, other)
    hi = ((c + RANKS // 2) % RANKS, other)
    sib = (c + 1 - 2 * core, t)
    prev = ((c + RANKS - 1) % RANKS, t)
    nxt = ((c + 1) % RANKS, t)
    far = ((c + RANKS - 1 + 2 * core) % RANKS, t)
    first = c == 0
    final = c == RANKS - 1
    before_seam = c == RANKS // 2 - 1
    after_seam = c == RANKS // 2
    inner = jnp.logical_not(first | final | before_seam | after_seam)

    barrier = pltpu.get_barrier_semaphore()

    def greet(peer):
        pl.semaphore_signal(barrier, inc=1, device_id=peer, device_id_type=MESH)

    for step in range(1, 8):
        greet((c, (t + step) % 8))
    greet(hi)
    greet(sib)

    @pl.when(inner)
    def _():
        greet(far)

    @pl.when(first)
    def _():
        greet((RANKS // 2 - 1, other))

    @pl.when(after_seam)
    def _():
        greet((RANKS - 1, other))

    lone = jnp.logical_or(first, after_seam)

    @pl.when(lone)
    def _():
        pl.semaphore_wait(barrier, 9)

    @pl.when(jnp.logical_not(lone))
    def _():
        pl.semaphore_wait(barrier, 10)

    @pl.when(before_seam)
    def _():
        pl.semaphore_signal(ready, inc=1, device_id=(0, other), device_id_type=MESH)

    def remote(src, dst, ss, rs, peer):
        return pltpu.make_async_remote_copy(
            src_ref=src, dst_ref=dst, send_sem=ss, recv_sem=rs,
            device_id=peer, device_id_type=MESH,
        )

    A = pl.ds(0, HALF)
    B = pl.ds(HALF, HALF)

    def slot(s, cols):
        return gbuf.at[pl.ds(s * PART, PART), cols]

    g_up_a = remote(g_hbm.at[:, A], slot(1, A), g_ss.at[0], g_rs.at[0], up)
    g_up_b = remote(g_hbm.at[:, B], slot(1, B), g_ss.at[1], g_rs.at[1], up)
    g_dn_b = remote(g_hbm.at[:, B], slot(2, B), g_ss.at[2], g_rs.at[2], down)
    g_dn_a = remote(g_hbm.at[:, A], slot(2, A), g_ss.at[3], g_rs.at[3], down)
    g_up_f, g_dn_f = [], []
    for i in range(2):
        ca = pl.ds(i * QUARTER, QUARTER)
        cb = pl.ds(HALF + i * QUARTER, QUARTER)
        g_up_f.append(remote(slot(1, ca), slot(3, ca), g_ss.at[4 + i], g_rs.at[4 + i], up))
        g_dn_f.append(remote(slot(2, cb), slot(3, cb), g_ss.at[6 + i], g_rs.at[6 + i], down))

    def wcols(link, k):
        return pl.ds(pl.multiple_of(core * 4096 + link * 2048 + k * SUB, SUB), SUB)

    w_sends, s_sends = [], []
    for k in range(2):
        for link, peer in ((0, lo), (1, hi)):
            i = 2 * k + link
            cols = wcols(link, k)
            w_sends.append(remote(w_hbm.at[:, cols], woth.at[:, cols], w_ss.at[i], w_rs.at[i], peer))
            s_sends.append(remote(woth.at[:, cols], woth.at[:, cols], s_ss.at[i], s_rs.at[i], sib))

    g_up_a.start()
    g_dn_b.start()
    w_sends[0].start()
    w_sends[1].start()
    g_up_b.start()
    g_dn_a.start()
    w_sends[2].start()
    w_sends[3].start()

    def back_ok(d):
        return jnp.logical_and(c >= 1, c + d <= RANKS - 1)

    def fwd_ok(d):
        return jnp.logical_and(c <= RANKS - 2, c - d >= 0)

    def q_copy(d):
        src = q_in if d == 0 else qw.at[d]
        return remote(src, qw.at[d + 1], q_ss.at[d], q_rs.at[d], prev)

    def l_copy(d):
        src = lse_in if d == 0 else lsew.at[d]
        return remote(src, lsew.at[d + 1], l_ss.at[d], l_rs.at[d], prev)

    def kv_copy(d):
        src = kv_in if d == 0 else kvw.at[d]
        return remote(src, kvw.at[d + 1], kv_ss.at[d], kv_rs.at[d], nxt)

    def do_copy(d, u):
        return remote(dow.at[d, u], dow.at[d + 1, u], do_ss.at[d, u], do_rs.at[d, u], prev)

    def de_copy(d):
        return remote(delw.at[d], delw.at[d + 1], de_ss.at[d], de_rs.at[d], prev)

    def q_src(d):
        return q_in if isinstance(d, int) and d == 0 else qw.at[d]

    def l_src(d):
        return lse_in if isinstance(d, int) and d == 0 else lsew.at[d]

    def kv_src(d):
        return kv_in if isinstance(d, int) and d == 0 else kvw.at[d]

    def send_q(d, when):
        ok = jnp.logical_and(when, back_ok(d))

        @pl.when(jnp.logical_and(ok, jnp.logical_not(after_seam)))
        def _():
            q_copy(d).start()
            l_copy(d).start()

        @pl.when(jnp.logical_and(ok, after_seam))
        def _():
            remote(q_src(d), rq.at[d], q_ss.at[d], rq_rs.at[d], hi).start()
            remote(l_src(d), rl.at[d], l_ss.at[d], rl_rs.at[d], hi).start()

    def send_kv(d, when):
        ok = jnp.logical_and(when, fwd_ok(d))

        @pl.when(jnp.logical_and(ok, jnp.logical_not(before_seam)))
        def _():
            kv_copy(d).start()

        @pl.when(jnp.logical_and(ok, before_seam))
        def _():
            remote(kv_src(d), rkv.at[d], kv_ss.at[d], rkv_rs.at[d], hi).start()

    def send_units(units, d, when):
        ok = jnp.logical_and(when, back_ok(d))

        @pl.when(jnp.logical_and(ok, jnp.logical_not(after_seam)))
        def _():
            for u in units:
                do_copy(d, u).start()

        @pl.when(jnp.logical_and(ok, after_seam))
        def _():
            for u in units:
                remote(dow.at[d, u], rdo.at[d, u], do_ss.at[d, u], rdo_rs.at[d, u], hi).start()

    def send_delta(d, when):
        ok = jnp.logical_and(when, back_ok(d))

        @pl.when(jnp.logical_and(ok, jnp.logical_not(after_seam)))
        def _():
            de_copy(d).start()

        @pl.when(jnp.logical_and(ok, after_seam))
        def _():
            remote(delw.at[d], rde.at[d], de_ss.at[d], rde_rs.at[d], hi).start()

    back_to = (RANKS // 2 - 1, other)
    on_to = (RANKS // 2, other)

    def relay_q(d):
        return (remote(rq.at[d], qw.at[d + 1], q_ss.at[d], q_rs.at[d], back_to),
                remote(rl.at[d], lsew.at[d + 1], l_ss.at[d], l_rs.at[d], back_to))

    def relay_q_in(d):
        return (remote(rq.at[d], rq.at[d], q_ss.at[d], rq_rs.at[d], hi),
                remote(rl.at[d], rl.at[d], l_ss.at[d], rl_rs.at[d], hi))

    def relay_units(units, d):
        for u in units:
            remote(rdo.at[d, u], rdo.at[d, u], do_ss.at[d, u], rdo_rs.at[d, u], hi).wait_recv()
            remote(rdo.at[d, u], dow.at[d + 1, u], do_ss.at[d, u], do_rs.at[d, u], back_to).start()

    def relay_delta(d):
        remote(rde.at[d], rde.at[d], de_ss.at[d], rde_rs.at[d], hi).wait_recv()
        remote(rde.at[d], delw.at[d + 1], de_ss.at[d], de_rs.at[d], back_to).start()

    def relay_kv(d):
        remote(rkv.at[d], rkv.at[d], kv_ss.at[d], rkv_rs.at[d], hi).wait_recv()
        remote(rkv.at[d], kvw.at[d + 1], kv_ss.at[d], kv_rs.at[d], on_to).start()

    send_q(0, True)
    send_kv(0, True)

    w_loc = pltpu.make_async_copy(w_hbm, wmine, loc_sem.at[0])
    g_loc = pltpu.make_async_copy(g_hbm, gbuf.at[pl.ds(0, PART), :], loc_sem.at[1])
    locals_ = [
        pltpu.make_async_copy(q_in, qw.at[0], loc_sem.at[2]),
        pltpu.make_async_copy(kv_in, kvw.at[0], loc_sem.at[3]),
        pltpu.make_async_copy(lse_in, lsew.at[0], loc_sem.at[4]),
        pltpu.make_async_copy(o_hbm, o_in, loc_sem.at[5]),
    ]
    w_loc.start()
    g_loc.start()
    for cp in locals_:
        cp.start()
    for d in range(1, REACH + 1):
        @pl.when(c + d > RANKS - 1)
        def _():
            qw[d] = jnp.zeros((ROWS, WIDE), BF16)
            lsew[d] = jnp.zeros((2, ROWS), F32)
            delw[d] = jnp.zeros((2, ROWS), F32)
            dow[d] = jnp.zeros((8, PART, WIDE), BF16)

        @pl.when(c - d < 0)
        def _():
            kvw[d] = jnp.zeros((ROWS, WIDE), BF16)

    def partial_product(first, count, w, starts, width):
        total = None
        for start in starts:
            cols = slice(start, start + width)
            one = lax.dot_general(
                gbuf[first * PART:(first + count) * PART, cols], w[:, cols], NT,
                preferred_element_type=F32)
            total = one if total is None else total + one
        return total

    even = (0, 2048, 4096, 6144)
    odd = (1024, 3072, 5120, 7168)
    slot_y = (y, (y + 3) % 4, (y + 1) % 4, (y + 2) % 4)
    own_unit = [xlo * 4 + v for v in slot_y]
    mate_unit = [(1 - xlo) * 4 + v for v in slot_y]
    early_units = own_unit[:3]
    middle_units = mate_unit[:3]
    late_units = [own_unit[3], mate_unit[3]]

    def mine(first, count):
        out = partial_product(first, count, wmine, (0,), D).astype(BF16)
        for s in range(first, first + count):
            dow[0, own_unit[s]] = out[(s - first) * PART:(s - first + 1) * PART]

    def x_copy(s):
        return remote(xsend.at[s], dow.at[0, own_unit[s]], x_ss.at[s], x_rs.at[s], lo)

    def forward_units(units, d):
        @pl.when(c + d <= RANKS - 1)
        def _():
            for u in units:
                do_copy(d - 1, u).wait_recv()

        send_units(units, d, True)

    def forward_kv(d, when):
        @pl.when(jnp.logical_and(when, c - d >= 0))
        def _():
            kv_copy(d - 1).wait_recv()

        send_kv(d, when)

    w_loc.wait()
    g_loc.wait()
    for cp in locals_:
        cp.wait()
    mine(0, 1)
    send_units(early_units[:1], 0, True)

    seam = RANKS // 2

    def q_over(d):
        return jnp.logical_and(c < seam, c + d >= seam)


    def kv_over(d):
        return jnp.logical_and(c >= seam, c - d < seam)


    def forward_q(d, when):
        @pl.when(jnp.logical_and(when, c + d <= RANKS - 1))
        def _():
            q_copy(d - 1).wait_recv()
            l_copy(d - 1).wait_recv()

        send_q(d, when)

    for d in range(1, REACH):
        forward_q(d, jnp.logical_not(q_over(d)))
        forward_kv(d, jnp.logical_not(kv_over(d)))

    g_up_a.wait_recv()
    g_dn_b.wait_recv()
    for i in range(2):
        g_up_f[i].start()
        g_dn_f[i].start()
    @pl.when(final)
    def _():
        for d in range(REACH):
            relay_kv(d)

    for h in range(2):
        lsec[h] = jnp.broadcast_to(lsew[0, h:h + 1, :], (HEAD, ROWS)).T
    for i in range(2):
        w_sends[i].wait_recv()
        s_sends[i].start()

    g_up_b.wait_recv()
    g_dn_a.wait_recv()
    mine(1, 2)

    send_units(early_units[1:], 0, True)
    for i in range(2):
        s_sends[i].wait_recv()
    acc_t[0:3 * PART, :] = partial_product(0, 3, woth, even, SUB)

    @pl.when(first)
    def _():
        pl.semaphore_wait(ready, 1)
        for d in range(REACH):
            for one, two in zip(relay_q_in(d), relay_q(d)):
                one.wait_recv()
                two.start()
        relay_units(mate_unit[:3], 0)

    forward_units(early_units, 1)
    forward_q(1, q_over(1))
    g_up_f[0].wait_recv()
    g_dn_f[0].wait_recv()
    acc_m[...] = partial_product(3, 1, wmine, (0, HALF), QUARTER)
    for i in range(2, 4):
        w_sends[i].wait_recv()
        s_sends[i].start()
    forward_units(early_units, 2)
    forward_q(2, q_over(2))
    for i in range(2, 4):
        s_sends[i].wait_recv()
    out = (acc_t[0:3 * PART, :] + partial_product(0, 3, woth, odd, SUB)).astype(BF16)
    for s in range(3):
        xsend[s] = out[s * PART:(s + 1) * PART]
        x_copy(s).start()
    acc_t[3 * PART:, :] = partial_product(3, 1, woth, (0, HALF), QUARTER)
    g_up_f[1].wait_recv()
    g_dn_f[1].wait_recv()
    later = (QUARTER, HALF + QUARTER)
    xsend[3] = (acc_t[3 * PART:, :] + partial_product(3, 1, woth, later, QUARTER)).astype(BF16)
    x_copy(3).start()
    for u in range(3):
        x_copy(u).wait_recv()
    send_units(middle_units, 0, True)
    dow[0, own_unit[3]] = (acc_m[...] + partial_product(3, 1, wmine, later, QUARTER)).astype(BF16)
    send_units(own_unit[3:], 0, True)
    forward_units(middle_units, 1)
    x_copy(3).wait_recv()
    send_units(mate_unit[3:], 0, True)

    ones = jnp.ones((8, HEAD), F32)
    for h in range(2):
        lanes = slice(h * HEAD, (h + 1) * HEAD)
        own = dow[0, :, :, lanes].reshape(ROWS, HEAD).astype(F32)
        prod = own * o_in[:, lanes].astype(F32)
        row = lax.dot_general(ones, prod, NT, precision=lax.Precision.HIGHEST,
                              preferred_element_type=F32)
        delw[0, h:h + 1, :] = row[0:1]
        delc[h] = jnp.broadcast_to(jnp.sum(prod, axis=1, keepdims=True), (ROWS, HEAD))

    send_delta(0, True)

    forward_units(early_units, 3)
    forward_q(3, q_over(3))
    for d in range(1, REACH):
        forward_kv(d, kv_over(d))

    lane_blk = lax.broadcasted_iota(jnp.int32, (1, ROWS), 1) // HEAD

    def bias_row(mine_doc, far_rank):
        vals = []
        for b in range(3):
            block = jnp.clip(far_rank * 3 + b, 0, 3 * RANKS - 1)
            inside = jnp.logical_and(far_rank >= 0, far_rank < RANKS)
            ok = jnp.logical_and(docs[block] == mine_doc, inside)
            vals.append(jnp.where(ok, 0.0, NEG).astype(F32))
        return jnp.where(lane_blk == 0, vals[0], jnp.where(lane_blk == 1, vals[1], vals[2]))

    def blocks(x):
        return [x[b * HEAD:(b + 1) * HEAD] for b in range(3)]

    def below():
        return (lax.broadcasted_iota(jnp.int32, (ROWS, ROWS), 0)
                <= lax.broadcasted_iota(jnp.int32, (ROWS, ROWS), 1))

    def key_side(d):
        k = kvw[0, :, 0:HEAD]
        v = kvw[0, :, HEAD:WIDE]
        rows = [bias_row(docs[c * 3 + b], c + d) for b in range(3)]
        for h in range(2):
            lanes = slice(h * HEAD, (h + 1) * HEAD)
            q = qw[d, :, lanes]
            do = dow[d, :, :, lanes].reshape(ROWS, HEAD)
            lse = lsew[d, h:h + 1, :]
            s = lax.dot_general(k, q, NT, preferred_element_type=F32)
            x = jnp.concatenate(
                [sb * SCALE + (row - lse) for sb, row in zip(blocks(s), rows)], axis=0)
            if isinstance(d, int) and d == 0:
                x = jnp.where(below(), x, NEG)
            p = jnp.exp(x)
            dp = lax.dot_general(v, do, NT, preferred_element_type=F32)
            ds = (p * (dp - delw[d, h:h + 1, :]) * SCALE).astype(BF16)
            dk = jnp.dot(ds, q, preferred_element_type=F32)
            dv = jnp.dot(p.astype(BF16), do, preferred_element_type=F32)
            if isinstance(d, int) and h == 0:
                dk_acc[...] = dk
                dv_acc[...] = dv
            else:
                dk_acc[...] += dk
                dv_acc[...] += dv

    def query_side(d):
        k = kvw[d, :, 0:HEAD]
        v = kvw[d, :, HEAD:WIDE]
        rows = [bias_row(docs[c * 3 + b], c - d) for b in range(3)]
        for h in range(2):
            lanes = slice(h * HEAD, (h + 1) * HEAD)
            q = qw[0, :, lanes]
            do = dow[0, :, :, lanes].reshape(ROWS, HEAD)
            lse = lsec[h]
            dl = delc[h]
            s = lax.dot_general(q, k, NT, preferred_element_type=F32)
            lse3 = jnp.concatenate([lse] * 3, axis=1)
            dl3 = jnp.concatenate([dl] * 3, axis=1)
            x = jnp.concatenate(
                [sb * SCALE + (row - lb) for sb, row, lb in zip(blocks(s), rows, blocks(lse3))],
                axis=0)
            if isinstance(d, int) and d == 0:
                x = jnp.where(jnp.logical_not(below()) | diagonal(), x, NEG)
            p = jnp.exp(x)
            dp = lax.dot_general(do, v, NT, preferred_element_type=F32)
            ds = (p * (dp - dl3) * SCALE).astype(BF16)
            dq = jnp.dot(ds, k, preferred_element_type=F32)
            if isinstance(d, int):
                dq_acc[h] = dq
            else:
                dq_acc[h] += dq

    def diagonal():
        return (lax.broadcasted_iota(jnp.int32, (ROWS, ROWS), 0)
                == lax.broadcasted_iota(jnp.int32, (ROWS, ROWS), 1))

    forward_units(middle_units, 2)

    @pl.when(first)
    def _():
        relay_units(own_unit[:3], 0)
        for d in range(1, 3):
            relay_units(mate_unit[:3], d)
        relay_units(own_unit[:3], 1)

    key_side(0)
    query_side(0)

    def chain_step(d, _):
        @pl.when(c + d <= RANKS - 1)
        def _():
            for u in late_units:
                do_copy(d - 1, u).wait_recv()
            de_copy(d - 1).wait_recv()

        @pl.when(jnp.logical_and(d == REACH - 1, c + d <= RANKS - 1))
        def _():
            for u in middle_units:
                do_copy(d - 1, u).wait_recv()

        send_units(middle_units, d, d == REACH - 1)
        send_units(late_units, d, True)
        send_delta(d, True)

        @pl.when(first)
        def _():
            relay_units([mate_unit[3], own_unit[3]], d - 1)
            relay_delta(d - 1)

        key_side(d)
        return 0

    last = REACH - 1

    @pl.when(c + REACH <= RANKS - 1)
    def _():
        q_copy(last).wait_recv()
        l_copy(last).wait_recv()
        for u in early_units:
            do_copy(last, u).wait_recv()

    lax.fori_loop(1, REACH, chain_step, 0)

    @pl.when(c + REACH <= RANKS - 1)
    def _():
        for u in middle_units + late_units:
            do_copy(last, u).wait_recv()
        de_copy(last).wait_recv()

    @pl.when(first)
    def _():
        relay_units(mate_unit[:3], 3)
        relay_units(own_unit[:3], 2)
        relay_units(own_unit[:3], 3)
        relay_units([mate_unit[3], own_unit[3]], 3)
        relay_delta(3)

    key_side(jnp.int32(REACH))

    part[:, 0:HEAD] = dk_acc[...].astype(BF16)
    part[:, HEAD:WIDE] = dv_acc[...].astype(BF16)

    def send(step):
        to = (t + step) % 8
        return remote(
            part.at[pl.ds(pl.multiple_of(to * PART, PART), PART)], land.at[step],
            r_ss.at[step], r_rs.at[step], (c, to))

    for step in range(1, 8):
        send(step).start()

    @pl.when(c - REACH >= 0)
    def _():
        kv_copy(last).wait_recv()

    def query_step(d, _):
        query_side(d)
        return 0

    lax.fori_loop(1, REACH + 1, query_step, 0)
    for h in range(2):
        dq_out[h] = dq_acc[h].astype(BF16)

    totals = [jnp.zeros((PART, WIDE), F32), jnp.zeros((PART, WIDE), F32)]
    for step in range(8):
        if step == 0:
            got = part[pl.ds(pl.multiple_of(t * PART, PART), PART), :].astype(F32)
        else:
            send(step).wait_recv()
            got = land[step].astype(F32)
        w1 = (((t + 8 - step) % 8) // 4).astype(F32)
        totals[0] = totals[0] + got * (1.0 - w1)
        totals[1] = totals[1] + got * w1
    for g in range(2):
        dkv_out[g] = totals[g].astype(BF16)

    for step in range(1, 8):
        send(step).wait_send()
    for cp in (g_up_a, g_up_b, g_dn_a, g_dn_b, *g_up_f, *g_dn_f, *w_sends, *s_sends):
        cp.wait_send()
    for s in range(4):
        x_copy(s).wait_send()
    for d in range(REACH):
        @pl.when(jnp.logical_or(first, back_ok(d)))
        def _():
            q_copy(d).wait_send()
            l_copy(d).wait_send()
            de_copy(d).wait_send()
            for u in range(8):
                do_copy(d, u).wait_send()

        @pl.when(jnp.logical_or(final, fwd_ok(d)))
        def _():
            kv_copy(d).wait_send()


def per_device(queries, key_tensor, value_tensor, attn_output, lse, grad_output, out_proj, block_doc):
    group = lax.axis_index("tp") // 4
    q2 = queries.reshape(ROWS, WIDE)
    o2 = attn_output.reshape(ROWS, WIDE)
    kv = jnp.concatenate(
        [
            lax.dynamic_index_in_dim(key_tensor, group, 1, keepdims=False),
            lax.dynamic_index_in_dim(value_tensor, group, 1, keepdims=False),
        ],
        axis=1,
    )
    vmem = pl.BlockSpec(memory_space=pltpu.VMEM)
    hbm = pl.BlockSpec(memory_space=pltpu.HBM)
    smem = pl.BlockSpec(memory_space=pltpu.SMEM)
    dma = pltpu.SemaphoreType.DMA
    span = REACH + 1
    dq, dkv = pl.pallas_call(
        fused_kernel,
        out_shape=(
            jax.ShapeDtypeStruct((2, ROWS, HEAD), BF16),
            jax.ShapeDtypeStruct((2, PART, WIDE), BF16),
        ),
        in_specs=[smem] + [hbm] * 6,
        out_specs=(vmem, vmem),
        scratch_shapes=[
            pltpu.VMEM((span, ROWS, WIDE), BF16),
            pltpu.VMEM((span, ROWS, WIDE), BF16),
            pltpu.VMEM((span, 2, ROWS), F32),
            pltpu.VMEM((span, 8, PART, WIDE), BF16),
            pltpu.VMEM((span, 2, ROWS), F32),
            pltpu.VMEM((ROWS, WIDE), BF16),
            pltpu.VMEM((2, ROWS, HEAD), F32),
            pltpu.VMEM((2, ROWS, HEAD), F32),
            pltpu.VMEM((WIDE, D), BF16),
            pltpu.VMEM((WIDE, D), BF16),
            pltpu.VMEM((4 * PART, D), BF16),
            pltpu.VMEM((4, PART, WIDE), BF16),
            pltpu.VMEM((4 * PART, WIDE), F32),
            pltpu.VMEM((PART, WIDE), F32),
            pltpu.VMEM((ROWS, HEAD), F32),
            pltpu.VMEM((ROWS, HEAD), F32),
            pltpu.VMEM((2, ROWS, HEAD), F32),
            pltpu.VMEM((ROWS, WIDE), BF16),
            pltpu.VMEM((8, PART, WIDE), BF16),
            dma((6,)), dma((8,)), dma((8,)), dma((4,)), dma((4,)), dma((4,)), dma((4,)),
            dma((4,)), dma((4,)), dma((4,)), dma((4,)), dma((4,)), dma((4,)),
            dma((4,)), dma((4,)), dma((4, 8)), dma((4, 8)), dma((4,)), dma((4,)),
            dma((8,)), dma((8,)), pltpu.SemaphoreType.REGULAR,
            pltpu.VMEM((REACH, ROWS, WIDE), BF16),
            pltpu.VMEM((REACH, 2, ROWS), F32),
            pltpu.VMEM((REACH, ROWS, WIDE), BF16),
            pltpu.VMEM((REACH, 8, PART, WIDE), BF16),
            pltpu.VMEM((REACH, 2, ROWS), F32),
            dma((4,)), dma((4,)), dma((4,)), dma((4, 8)), dma((4,)),
        ],
        compiler_params=pltpu.CompilerParams(
            collective_id=0, has_side_effects=True, vmem_limit_bytes=67043328 - 720 * 1024),
        name="attention_backward",
    )(block_doc, q2, kv, lse, o2, grad_output, out_proj)
    grad_query = jnp.transpose(dq, (1, 0, 2))
    grad_key = jnp.transpose(dkv[:, :, :HEAD], (1, 0, 2))
    grad_value = jnp.transpose(dkv[:, :, HEAD:], (1, 0, 2))
    return grad_query, grad_key, grad_value


def solution(mesh):
    placed = (
        P("ctx", "tp", None),
        P("ctx", None, None),
        P("ctx", None, None),
        P("ctx", "tp", None),
        P("tp", "ctx"),
        P(("ctx", "tp"), None),
        P("tp", None),
        P(),
    )
    return jax.shard_map(
        per_device,
        mesh=mesh,
        in_specs=placed,
        out_specs=(
            P("ctx", "tp", None),
            P(("ctx", "tp"), None, None),
            P(("ctx", "tp"), None, None),
        ),
        check_vma=False,
    )
```

```python
import jax
import jax.numpy as jnp
from jax import lax
from jax.experimental import pallas as pl
from jax.experimental.pallas import tpu as pltpu
from jax.sharding import PartitionSpec as P

F32 = jnp.float32
BF16 = jnp.bfloat16
MESH = pl.DeviceIdType.MESH
RANKS = 128
REACH = 4
ROWS = 384
PART = 48
HEAD = 128
WIDE = 256
D = 8192
HALF = D // 2
QUARTER = D // 4
SUB = D // 8
NEG = -1e30
SCALE = HEAD ** -0.5
NT = (((1,), (1,)), ((), ()))


def ring_places():
    c = lax.axis_index("ctx")
    t = lax.axis_index("tp")
    return c, t


def fused_kernel(
    docs, q_in, k_in, v_in, lse_in, o_hbm, g_hbm, w_hbm,
    dq_out, dkv_out,
    qw, kvw, lsew, dow, delw, o_in, lsec, delc,
    wmine, woth, gbuf, xsend, acc_t, acc_m, dk_acc, dv_acc, dq_acc, part, land,
    loc_sem, g_ss, g_rs, w_ss, w_rs, s_ss, s_rs,
    q_ss, q_rs, l_ss, l_rs, kv_ss, kv_rs, x_ss, x_rs, do_ss, do_rs, de_ss, de_rs,
    r_ss, r_rs, ready,
    rq, rl, rkv, rdo, rde, rq_rs, rl_rs, rkv_rs, rdo_rs, rde_rs,
):
    c, t = ring_places()
    xlo = t // 4
    y = t % 4
    core = c % 2
    up = (c, xlo * 4 + (y + 1) % 4)
    down = (c, xlo * 4 + (y + 3) % 4)
    other = (t + 4) % 8
    lo = (c, other)
    hi = ((c + RANKS // 2) % RANKS, other)
    sib = (c + 1 - 2 * core, t)
    prev = ((c + RANKS - 1) % RANKS, t)
    nxt = ((c + 1) % RANKS, t)
    far = ((c + RANKS - 1 + 2 * core) % RANKS, t)
    first = c == 0
    final = c == RANKS - 1
    before_seam = c == RANKS // 2 - 1
    after_seam = c == RANKS // 2
    inner = jnp.logical_not(first | final | before_seam | after_seam)

    barrier = pltpu.get_barrier_semaphore()

    def greet(peer):
        pl.semaphore_signal(barrier, inc=1, device_id=peer, device_id_type=MESH)

    for step in range(1, 8):
        greet((c, (t + step) % 8))
    greet(hi)
    greet(sib)

    @pl.when(inner)
    def _():
        greet(far)

    @pl.when(first)
    def _():
        greet((RANKS // 2 - 1, other))

    @pl.when(after_seam)
    def _():
        greet((RANKS - 1, other))

    lone = jnp.logical_or(first, after_seam)

    @pl.when(lone)
    def _():
        pl.semaphore_wait(barrier, 9)

    @pl.when(jnp.logical_not(lone))
    def _():
        pl.semaphore_wait(barrier, 10)

    @pl.when(before_seam)
    def _():
        pl.semaphore_signal(ready, inc=1, device_id=(0, other), device_id_type=MESH)

    def remote(src, dst, ss, rs, peer):
        return pltpu.make_async_remote_copy(
            src_ref=src, dst_ref=dst, send_sem=ss, recv_sem=rs,
            device_id=peer, device_id_type=MESH,
        )

    A = pl.ds(0, HALF)
    B = pl.ds(HALF, HALF)

    def slot(s, cols):
        return gbuf.at[pl.ds(s * PART, PART), cols]

    g_up_a = remote(g_hbm.at[:, A], slot(1, A), g_ss.at[0], g_rs.at[0], up)
    g_up_b = remote(g_hbm.at[:, B], slot(1, B), g_ss.at[1], g_rs.at[1], up)
    g_dn_b = remote(g_hbm.at[:, B], slot(2, B), g_ss.at[2], g_rs.at[2], down)
    g_dn_a = remote(g_hbm.at[:, A], slot(2, A), g_ss.at[3], g_rs.at[3], down)
    g_up_f, g_dn_f = [], []
    for i in range(2):
        ca = pl.ds(i * QUARTER, QUARTER)
        cb = pl.ds(HALF + i * QUARTER, QUARTER)
        g_up_f.append(remote(slot(1, ca), slot(3, ca), g_ss.at[4 + i], g_rs.at[4 + i], up))
        g_dn_f.append(remote(slot(2, cb), slot(3, cb), g_ss.at[6 + i], g_rs.at[6 + i], down))

    def wcols(link, k):
        return pl.ds(pl.multiple_of(core * 4096 + link * 2048 + k * SUB, SUB), SUB)

    w_sends, s_sends = [], []
    for k in range(2):
        for link, peer in ((0, lo), (1, hi)):
            i = 2 * k + link
            cols = wcols(link, k)
            w_sends.append(remote(w_hbm.at[:, cols], woth.at[:, cols], w_ss.at[i], w_rs.at[i], peer))
            s_sends.append(remote(woth.at[:, cols], woth.at[:, cols], s_ss.at[i], s_rs.at[i], sib))

    g_up_a.start()
    g_dn_b.start()
    w_sends[0].start()
    w_sends[1].start()
    g_up_b.start()
    g_dn_a.start()
    w_sends[2].start()
    w_sends[3].start()

    def back_ok(d):
        return jnp.logical_and(c >= 1, c + d <= RANKS - 1)

    def fwd_ok(d):
        return jnp.logical_and(c <= RANKS - 2, c - d >= 0)

    def q_copy(d):
        src = q_in if d == 0 else qw.at[d]
        return remote(src, qw.at[d + 1], q_ss.at[d], q_rs.at[d], prev)

    def l_copy(d):
        src = lse_in if d == 0 else lsew.at[d]
        return remote(src, lsew.at[d + 1], l_ss.at[d], l_rs.at[d], prev)

    def kv_copy(d):
        return remote(kvw.at[d], kvw.at[d + 1], kv_ss.at[d], kv_rs.at[d], nxt)

    def do_copy(d, u):
        return remote(dow.at[d, u], dow.at[d + 1, u], do_ss.at[d, u], do_rs.at[d, u], prev)

    def de_copy(d):
        return remote(delw.at[d], delw.at[d + 1], de_ss.at[d], de_rs.at[d], prev)

    def q_src(d):
        return q_in if isinstance(d, int) and d == 0 else qw.at[d]

    def l_src(d):
        return lse_in if isinstance(d, int) and d == 0 else lsew.at[d]

    def kv_src(d):
        return kvw.at[d]

    def send_q(d, when):
        ok = jnp.logical_and(when, back_ok(d))

        @pl.when(jnp.logical_and(ok, jnp.logical_not(after_seam)))
        def _():
            q_copy(d).start()
            l_copy(d).start()

        @pl.when(jnp.logical_and(ok, after_seam))
        def _():
            remote(q_src(d), rq.at[d], q_ss.at[d], rq_rs.at[d], hi).start()
            remote(l_src(d), rl.at[d], l_ss.at[d], rl_rs.at[d], hi).start()

    def send_kv(d, when):
        ok = jnp.logical_and(when, fwd_ok(d))

        @pl.when(jnp.logical_and(ok, jnp.logical_not(before_seam)))
        def _():
            kv_copy(d).start()

        @pl.when(jnp.logical_and(ok, before_seam))
        def _():
            remote(kv_src(d), rkv.at[d], kv_ss.at[d], rkv_rs.at[d], hi).start()

    def send_units(units, d, when):
        ok = jnp.logical_and(when, back_ok(d))

        @pl.when(jnp.logical_and(ok, jnp.logical_not(after_seam)))
        def _():
            for u in units:
                do_copy(d, u).start()

        @pl.when(jnp.logical_and(ok, after_seam))
        def _():
            for u in units:
                remote(dow.at[d, u], rdo.at[d, u], do_ss.at[d, u], rdo_rs.at[d, u], hi).start()

    def send_delta(d, when):
        ok = jnp.logical_and(when, back_ok(d))

        @pl.when(jnp.logical_and(ok, jnp.logical_not(after_seam)))
        def _():
            de_copy(d).start()

        @pl.when(jnp.logical_and(ok, after_seam))
        def _():
            remote(delw.at[d], rde.at[d], de_ss.at[d], rde_rs.at[d], hi).start()

    back_to = (RANKS // 2 - 1, other)
    on_to = (RANKS // 2, other)

    def relay_q(d):
        return (remote(rq.at[d], qw.at[d + 1], q_ss.at[d], q_rs.at[d], back_to),
                remote(rl.at[d], lsew.at[d + 1], l_ss.at[d], l_rs.at[d], back_to))

    def relay_q_in(d):
        return (remote(rq.at[d], rq.at[d], q_ss.at[d], rq_rs.at[d], hi),
                remote(rl.at[d], rl.at[d], l_ss.at[d], rl_rs.at[d], hi))

    def relay_units(units, d):
        for u in units:
            remote(rdo.at[d, u], rdo.at[d, u], do_ss.at[d, u], rdo_rs.at[d, u], hi).wait_recv()
            remote(rdo.at[d, u], dow.at[d + 1, u], do_ss.at[d, u], do_rs.at[d, u], back_to).start()

    def relay_delta(d):
        remote(rde.at[d], rde.at[d], de_ss.at[d], rde_rs.at[d], hi).wait_recv()
        remote(rde.at[d], delw.at[d + 1], de_ss.at[d], de_rs.at[d], back_to).start()

    def relay_kv(d):
        remote(rkv.at[d], rkv.at[d], kv_ss.at[d], rkv_rs.at[d], hi).wait_recv()
        remote(rkv.at[d], kvw.at[d + 1], kv_ss.at[d], kv_rs.at[d], on_to).start()

    send_q(0, True)

    w_loc = pltpu.make_async_copy(w_hbm, wmine, loc_sem.at[0])
    g_loc = pltpu.make_async_copy(g_hbm, gbuf.at[pl.ds(0, PART), :], loc_sem.at[1])
    group = pl.ds(pl.multiple_of(xlo * HEAD, HEAD), HEAD)
    locals_ = [
        pltpu.make_async_copy(q_in, qw.at[0], loc_sem.at[2]),
        pltpu.make_async_copy(k_in.at[:, group], kvw.at[0, :, pl.ds(0, HEAD)], loc_sem.at[3]),
        pltpu.make_async_copy(v_in.at[:, group], kvw.at[0, :, pl.ds(HEAD, HEAD)], loc_sem.at[6]),
        pltpu.make_async_copy(lse_in, lsew.at[0], loc_sem.at[4]),
        pltpu.make_async_copy(o_hbm, o_in, loc_sem.at[5]),
    ]
    for cp in locals_:
        cp.start()
    w_loc.start()
    g_loc.start()
    for d in range(1, REACH + 1):
        @pl.when(c + d > RANKS - 1)
        def _():
            qw[d] = jnp.zeros((ROWS, WIDE), BF16)
            lsew[d] = jnp.zeros((2, ROWS), F32)
            delw[d] = jnp.zeros((2, ROWS), F32)
            dow[d] = jnp.zeros((8, PART, WIDE), BF16)

        @pl.when(c - d < 0)
        def _():
            kvw[d] = jnp.zeros((ROWS, WIDE), BF16)

    def partial_product(first, count, w, starts, width):
        total = None
        for start in starts:
            cols = slice(start, start + width)
            one = lax.dot_general(
                gbuf[first * PART:(first + count) * PART, cols], w[:, cols], NT,
                preferred_element_type=F32)
            total = one if total is None else total + one
        return total

    even = (0, 2048, 4096, 6144)
    odd = (1024, 3072, 5120, 7168)
    slot_y = (y, (y + 3) % 4, (y + 1) % 4, (y + 2) % 4)
    own_unit = [xlo * 4 + v for v in slot_y]
    mate_unit = [(1 - xlo) * 4 + v for v in slot_y]
    early_units = own_unit[:3]
    middle_units = mate_unit[:3]
    late_units = [own_unit[3], mate_unit[3]]

    def mine(first, count):
        out = partial_product(first, count, wmine, (0,), D).astype(BF16)
        for s in range(first, first + count):
            dow[0, own_unit[s]] = out[(s - first) * PART:(s - first + 1) * PART]

    def x_copy(s):
        return remote(xsend.at[s], dow.at[0, own_unit[s]], x_ss.at[s], x_rs.at[s], lo)

    def forward_units(units, d):
        @pl.when(c + d <= RANKS - 1)
        def _():
            for u in units:
                do_copy(d - 1, u).wait_recv()

        send_units(units, d, True)

    def forward_kv(d, when):
        @pl.when(jnp.logical_and(when, c - d >= 0))
        def _():
            kv_copy(d - 1).wait_recv()

        send_kv(d, when)

    for cp in locals_:
        cp.wait()
    send_kv(0, True)
    w_loc.wait()
    g_loc.wait()
    mine(0, 1)
    send_units(early_units[:1], 0, True)

    seam = RANKS // 2

    def q_over(d):
        return jnp.logical_and(c < seam, c + d >= seam)


    def kv_over(d):
        return jnp.logical_and(c >= seam, c - d < seam)


    def forward_q(d, when):
        @pl.when(jnp.logical_and(when, c + d <= RANKS - 1))
        def _():
            q_copy(d - 1).wait_recv()
            l_copy(d - 1).wait_recv()

        send_q(d, when)

    for d in range(1, REACH):
        forward_q(d, jnp.logical_not(q_over(d)))
        forward_kv(d, jnp.logical_not(kv_over(d)))

    g_up_a.wait_recv()
    g_dn_b.wait_recv()
    for i in range(2):
        g_up_f[i].start()
        g_dn_f[i].start()
    @pl.when(final)
    def _():
        for d in range(REACH):
            relay_kv(d)

    for h in range(2):
        lsec[h] = jnp.broadcast_to(lsew[0, h:h + 1, :], (HEAD, ROWS)).T
    for i in range(2):
        w_sends[i].wait_recv()
        s_sends[i].start()

    g_up_b.wait_recv()
    g_dn_a.wait_recv()
    mine(1, 2)

    send_units(early_units[1:], 0, True)
    for i in range(2):
        s_sends[i].wait_recv()
    acc_t[0:3 * PART, :] = partial_product(0, 3, woth, even, SUB)

    forward_units(early_units, 1)
    forward_q(1, q_over(1))
    g_up_f[0].wait_recv()
    g_dn_f[0].wait_recv()
    acc_m[...] = partial_product(3, 1, wmine, (0, HALF), QUARTER)
    for i in range(2, 4):
        w_sends[i].wait_recv()
        s_sends[i].start()
    forward_units(early_units, 2)
    forward_q(2, q_over(2))
    for i in range(2, 4):
        s_sends[i].wait_recv()

    def hand_on_q(d):
        for one, two in zip(relay_q_in(d), relay_q(d)):
            one.wait_recv()
            two.start()

    @pl.when(first)
    def _():
        pl.semaphore_wait(ready, 1)
        hand_on_q(0)
        relay_units(mate_unit[:3], 0)
        for d in range(1, REACH):
            hand_on_q(d)

    out = (acc_t[0:3 * PART, :] + partial_product(0, 3, woth, odd, SUB)).astype(BF16)
    for s in range(3):
        xsend[s] = out[s * PART:(s + 1) * PART]
        x_copy(s).start()
    acc_t[3 * PART:, :] = partial_product(3, 1, woth, (0, HALF), QUARTER)
    g_up_f[1].wait_recv()
    g_dn_f[1].wait_recv()
    later = (QUARTER, HALF + QUARTER)
    xsend[3] = (acc_t[3 * PART:, :] + partial_product(3, 1, woth, later, QUARTER)).astype(BF16)
    x_copy(3).start()
    for u in range(3):
        x_copy(u).wait_recv()
    send_units(middle_units, 0, True)
    dow[0, own_unit[3]] = (acc_m[...] + partial_product(3, 1, wmine, later, QUARTER)).astype(BF16)
    send_units(own_unit[3:], 0, True)
    forward_units(middle_units, 1)
    x_copy(3).wait_recv()
    send_units(mate_unit[3:], 0, True)

    ones = jnp.ones((8, HEAD), F32)
    for h in range(2):
        lanes = slice(h * HEAD, (h + 1) * HEAD)
        own = dow[0, :, :, lanes].reshape(ROWS, HEAD).astype(F32)
        prod = own * o_in[:, lanes].astype(F32)
        row = lax.dot_general(ones, prod, NT, precision=lax.Precision.HIGHEST,
                              preferred_element_type=F32)
        delw[0, h:h + 1, :] = row[0:1]
        delc[h] = jnp.broadcast_to(jnp.sum(prod, axis=1, keepdims=True), (ROWS, HEAD))

    send_delta(0, True)

    forward_units(early_units, 3)
    forward_q(3, q_over(3))

    lane_blk = lax.broadcasted_iota(jnp.int32, (1, ROWS), 1) // HEAD

    def bias_row(mine_doc, far_rank):
        vals = []
        for b in range(3):
            block = jnp.clip(far_rank * 3 + b, 0, 3 * RANKS - 1)
            inside = jnp.logical_and(far_rank >= 0, far_rank < RANKS)
            ok = jnp.logical_and(docs[block] == mine_doc, inside)
            vals.append(jnp.where(ok, 0.0, NEG).astype(F32))
        return jnp.where(lane_blk == 0, vals[0], jnp.where(lane_blk == 1, vals[1], vals[2]))

    def blocks(x):
        return [x[b * HEAD:(b + 1) * HEAD] for b in range(3)]

    def below():
        return (lax.broadcasted_iota(jnp.int32, (ROWS, ROWS), 0)
                <= lax.broadcasted_iota(jnp.int32, (ROWS, ROWS), 1))

    def key_side(d):
        k = kvw[0, :, 0:HEAD]
        v = kvw[0, :, HEAD:WIDE]
        rows = [bias_row(docs[c * 3 + b], c + d) for b in range(3)]
        for h in range(2):
            lanes = slice(h * HEAD, (h + 1) * HEAD)
            q = qw[d, :, lanes]
            do = dow[d, :, :, lanes].reshape(ROWS, HEAD)
            lse = lsew[d, h:h + 1, :]
            s = lax.dot_general(k, q, NT, preferred_element_type=F32)
            x = jnp.concatenate(
                [sb * SCALE + (row - lse) for sb, row in zip(blocks(s), rows)], axis=0)
            if isinstance(d, int) and d == 0:
                x = jnp.where(below(), x, NEG)
            p = jnp.exp(x)
            dp = lax.dot_general(v, do, NT, preferred_element_type=F32)
            ds = (p * (dp - delw[d, h:h + 1, :]) * SCALE).astype(BF16)
            dk = jnp.dot(ds, q, preferred_element_type=F32)
            dv = jnp.dot(p.astype(BF16), do, preferred_element_type=F32)
            if isinstance(d, int) and h == 0:
                dk_acc[...] = dk
                dv_acc[...] = dv
            else:
                dk_acc[...] += dk
                dv_acc[...] += dv

    def query_side(d):
        k = kvw[d, :, 0:HEAD]
        v = kvw[d, :, HEAD:WIDE]
        rows = [bias_row(docs[c * 3 + b], c - d) for b in range(3)]
        for h in range(2):
            lanes = slice(h * HEAD, (h + 1) * HEAD)
            q = qw[0, :, lanes]
            do = dow[0, :, :, lanes].reshape(ROWS, HEAD)
            lse = lsec[h]
            dl = delc[h]
            s = lax.dot_general(q, k, NT, preferred_element_type=F32)
            lse3 = jnp.concatenate([lse] * 3, axis=1)
            dl3 = jnp.concatenate([dl] * 3, axis=1)
            x = jnp.concatenate(
                [sb * SCALE + (row - lb) for sb, row, lb in zip(blocks(s), rows, blocks(lse3))],
                axis=0)
            if isinstance(d, int) and d == 0:
                x = jnp.where(jnp.logical_not(below()) | diagonal(), x, NEG)
            p = jnp.exp(x)
            dp = lax.dot_general(do, v, NT, preferred_element_type=F32)
            ds = (p * (dp - dl3) * SCALE).astype(BF16)
            dq = jnp.dot(ds, k, preferred_element_type=F32)
            if isinstance(d, int):
                dq_acc[h] = dq
            else:
                dq_acc[h] += dq

    def diagonal():
        return (lax.broadcasted_iota(jnp.int32, (ROWS, ROWS), 0)
                == lax.broadcasted_iota(jnp.int32, (ROWS, ROWS), 1))

    key_side(0)

    @pl.when(first)
    def _():
        relay_units(own_unit[:3], 0)
        for d in range(1, 3):
            relay_units(mate_unit[:3], d)
        relay_units(own_unit[:3], 1)


    def chain_step(d, _):
        @pl.when(c + d <= RANKS - 1)
        def _():
            for u in late_units:
                do_copy(d - 1, u).wait_recv()
            de_copy(d - 1).wait_recv()

        send_units(late_units, d, True)
        send_delta(d, True)

        @pl.when(jnp.logical_and(d < REACH - 1, c + d + 1 <= RANKS - 1))
        def _():
            for u in middle_units:
                do_copy(d, u).wait_recv()

        send_units(middle_units, d + 1, d < REACH - 1)

        @pl.when(first)
        def _():
            relay_units([mate_unit[3], own_unit[3]], d - 1)
            relay_delta(d - 1)

        key_side(d)
        return 0

    last = REACH - 1

    @pl.when(c + REACH <= RANKS - 1)
    def _():
        q_copy(last).wait_recv()
        l_copy(last).wait_recv()
        for u in early_units:
            do_copy(last, u).wait_recv()

    chain_step(jnp.int32(1), 0)
    query_side(0)
    lax.fori_loop(2, REACH, chain_step, 0)

    @pl.when(c + REACH <= RANKS - 1)
    def _():
        for u in middle_units + late_units:
            do_copy(last, u).wait_recv()
        de_copy(last).wait_recv()

    @pl.when(first)
    def _():
        relay_units(mate_unit[:3], 3)
        relay_units(own_unit[:3], 2)
        relay_units(own_unit[:3], 3)
        relay_units([mate_unit[3], own_unit[3]], 3)
        relay_delta(3)

    key_side(jnp.int32(REACH))

    part[:, 0:HEAD] = dk_acc[...].astype(BF16)
    part[:, HEAD:WIDE] = dv_acc[...].astype(BF16)

    def send(step):
        to = (t + step) % 8
        return remote(
            part.at[pl.ds(pl.multiple_of(to * PART, PART), PART)], land.at[step],
            r_ss.at[step], r_rs.at[step], (c, to))

    for step in range(1, 8):
        send(step).start()

    for d in range(1, REACH):
        forward_kv(d, kv_over(d))

    @pl.when(c - REACH >= 0)
    def _():
        kv_copy(last).wait_recv()

    def query_step(d, _):
        query_side(d)
        return 0

    lax.fori_loop(1, REACH + 1, query_step, 0)
    for h in range(2):
        dq_out[h] = dq_acc[h].astype(BF16)

    totals = [jnp.zeros((PART, WIDE), F32), jnp.zeros((PART, WIDE), F32)]
    for step in range(8):
        if step == 0:
            got = part[pl.ds(pl.multiple_of(t * PART, PART), PART), :].astype(F32)
        else:
            send(step).wait_recv()
            got = land[step].astype(F32)
        w1 = (((t + 8 - step) % 8) // 4).astype(F32)
        totals[0] = totals[0] + got * (1.0 - w1)
        totals[1] = totals[1] + got * w1
    for g in range(2):
        dkv_out[g] = totals[g].astype(BF16)

    for step in range(1, 8):
        send(step).wait_send()
    for cp in (g_up_a, g_up_b, g_dn_a, g_dn_b, *g_up_f, *g_dn_f, *w_sends, *s_sends):
        cp.wait_send()
    for s in range(4):
        x_copy(s).wait_send()
    for d in range(REACH):
        @pl.when(jnp.logical_or(first, back_ok(d)))
        def _():
            q_copy(d).wait_send()
            l_copy(d).wait_send()
            de_copy(d).wait_send()
            for u in range(8):
                do_copy(d, u).wait_send()

        @pl.when(jnp.logical_or(final, fwd_ok(d)))
        def _():
            kv_copy(d).wait_send()


def per_device(queries, key_tensor, value_tensor, attn_output, lse, grad_output, out_proj, block_doc):
    q2 = queries.reshape(ROWS, WIDE)
    k2 = key_tensor.reshape(ROWS, WIDE)
    v2 = value_tensor.reshape(ROWS, WIDE)
    o2 = attn_output.reshape(ROWS, WIDE)
    vmem = pl.BlockSpec(memory_space=pltpu.VMEM)
    hbm = pl.BlockSpec(memory_space=pltpu.HBM)
    smem = pl.BlockSpec(memory_space=pltpu.SMEM)
    dma = pltpu.SemaphoreType.DMA
    span = REACH + 1
    dq, dkv = pl.pallas_call(
        fused_kernel,
        out_shape=(
            jax.ShapeDtypeStruct((2, ROWS, HEAD), BF16),
            jax.ShapeDtypeStruct((2, PART, WIDE), BF16),
        ),
        in_specs=[smem] + [hbm] * 7,
        out_specs=(vmem, vmem),
        scratch_shapes=[
            pltpu.VMEM((span, ROWS, WIDE), BF16),
            pltpu.VMEM((span, ROWS, WIDE), BF16),
            pltpu.VMEM((span, 2, ROWS), F32),
            pltpu.VMEM((span, 8, PART, WIDE), BF16),
            pltpu.VMEM((span, 2, ROWS), F32),
            pltpu.VMEM((ROWS, WIDE), BF16),
            pltpu.VMEM((2, ROWS, HEAD), F32),
            pltpu.VMEM((2, ROWS, HEAD), F32),
            pltpu.VMEM((WIDE, D), BF16),
            pltpu.VMEM((WIDE, D), BF16),
            pltpu.VMEM((4 * PART, D), BF16),
            pltpu.VMEM((4, PART, WIDE), BF16),
            pltpu.VMEM((4 * PART, WIDE), F32),
            pltpu.VMEM((PART, WIDE), F32),
            pltpu.VMEM((ROWS, HEAD), F32),
            pltpu.VMEM((ROWS, HEAD), F32),
            pltpu.VMEM((2, ROWS, HEAD), F32),
            pltpu.VMEM((ROWS, WIDE), BF16),
            pltpu.VMEM((8, PART, WIDE), BF16),
            dma((7,)), dma((8,)), dma((8,)), dma((4,)), dma((4,)), dma((4,)), dma((4,)),
            dma((4,)), dma((4,)), dma((4,)), dma((4,)), dma((4,)), dma((4,)),
            dma((4,)), dma((4,)), dma((4, 8)), dma((4, 8)), dma((4,)), dma((4,)),
            dma((8,)), dma((8,)), pltpu.SemaphoreType.REGULAR,
            pltpu.VMEM((REACH, ROWS, WIDE), BF16),
            pltpu.VMEM((REACH, 2, ROWS), F32),
            pltpu.VMEM((REACH, ROWS, WIDE), BF16),
            pltpu.VMEM((REACH, 8, PART, WIDE), BF16),
            pltpu.VMEM((REACH, 2, ROWS), F32),
            dma((4,)), dma((4,)), dma((4,)), dma((4, 8)), dma((4,)),
        ],
        compiler_params=pltpu.CompilerParams(
            collective_id=0, has_side_effects=True, vmem_limit_bytes=53 << 20),
        name="attention_backward",
    )(block_doc, q2, k2, v2, lse, o2, grad_output, out_proj)
    grad_query = jnp.transpose(dq, (1, 0, 2))
    grad_key = jnp.transpose(dkv[:, :, :HEAD], (1, 0, 2))
    grad_value = jnp.transpose(dkv[:, :, HEAD:], (1, 0, 2))
    return grad_query, grad_key, grad_value


def solution(mesh):
    placed = (
        P("ctx", "tp", None),
        P("ctx", None, None),
        P("ctx", None, None),
        P("ctx", "tp", None),
        P("tp", "ctx"),
        P(("ctx", "tp"), None),
        P("tp", None),
        P(),
    )
    return jax.shard_map(
        per_device,
        mesh=mesh,
        in_specs=placed,
        out_specs=(
            P("ctx", "tp", None),
            P(("ctx", "tp"), None, None),
            P(("ctx", "tp"), None, None),
        ),
        check_vma=False,
    )
```
